32 devices in a mesh: row: 4 (over z), col: 8 (over y, x, core).
Axes of the slice: x: 2, y: 2, z: 4, core: 2. Of those that a mesh axis runs over, the one named last changes fastest.
Arguments:
- base_flat: bfloat16 [2, 29568, 8192], P(None, ('row', 'col')), may hold values from -6 to 6
- adjusted_flat: bfloat16 [2, 29568, 8192], P(None, ('row', 'col')), may hold values from -6 to 6
- omega: bfloat16 [2, 8192, 256], P(None, 'col'), may hold values from -6 to 6
Outputs:
- adapter_up_basis: float32 [2, 29568, 256], P(None, ('row', 'col'))
- adapter_down_transposed: float32 [2, 8192, 256], P(None, 'col', 'row')
The draws below stay inside these ranges and needn't reach their ends.
All inputs are finite; a program needn't handle non-finite values.
Results may differ from the reference program's by a relative error of at most 0.011.
Values may be sent and summed in bfloat16 or wider, within the bound.
No kernel may reach another device: no remote copies, remote signals or barrier semaphores. Data moves between devices by JAX's collectives and lax.ppermute only.
A program may use at most 192 MiB of HBM per device.

```python
import math
import jax
import jax.numpy as jnp
from jax import lax

HIDDEN_UNITS = 29568
N = 8192
K = 256
MATS = 2


def levels(stream_key, dims, split, smallest, top_value):
    factor_of = 1.0
    for dim, parts in split:
        steps = jax.random.uniform(jax.random.fold_in(jax.random.fold_in(stream_key, 6), dim), (parts,), jnp.float32, smallest / len(split), top_value / len(split))
        factor_of = factor_of * jnp.repeat(jnp.exp(steps), dims[dim] // parts).reshape((-1,) + (1,) * (len(dims) - 1 - dim))
    return factor_of


def gaussian(key, dims, spread, reach, pieces=(), kind=jnp.bfloat16):
    values = jax.random.normal(key, dims, jnp.float32) * spread
    if len(pieces) > 0:
        values = levels(key, dims, pieces, -0.22, 0.18) * values
    return jnp.clip(values, min=-reach, max=reach).astype(kind)


def setup_inputs(seed: int = 0) -> dict:
    streams_of = jax.random.split(jax.random.key(seed), 4)
    return {
        "base_flat": gaussian(streams_of[0], (MATS, HIDDEN_UNITS, N), 1.0, 6.0, ((1, 32),)),
        "adjusted_flat": gaussian(streams_of[1], (MATS, HIDDEN_UNITS, N), 1.0, 6.0, ((1, 32),)),
        "omega": gaussian(streams_of[2], (MATS, N, K), 1.0, 6.0, ((1, 8),)),
    }


def product(left, right):
    return jnp.dot(left.astype(jnp.float32), right.astype(jnp.float32), precision=lax.Precision.HIGHEST)

def orthonormal(panel):
    gram = jnp.dot(panel.T, panel, precision=lax.Precision.HIGHEST)
    lower = jnp.linalg.cholesky(gram)
    solved = jax.scipy.linalg.solve_triangular(lower, panel.T, lower=True)
    return solved.T

def reference(base_flat, adjusted_flat, omega):
    ups = []
    downs = []
    for index in range(MATS):
        delta = (adjusted_flat[index].astype(jnp.float32) - base_flat[index].astype(jnp.float32)).astype(jnp.bfloat16)
        sketch = product(delta, omega[index])
        first_basis = orthonormal(sketch).astype(jnp.bfloat16)
        columns = product(delta.T, first_basis).astype(jnp.bfloat16)
        power = product(delta, columns)
        basis = orthonormal(power)
        ups.append(math.sqrt(HIDDEN_UNITS) * basis)
        downs.append(product(delta.T, basis.astype(jnp.bfloat16)))
    return (jnp.stack(ups), jnp.stack(downs))
```

```python
import functools
import math

import jax
import jax.numpy as jnp
from jax import lax
from jax.experimental import pallas as pl
from jax.experimental.pallas import tpu as pltpu
from jax.sharding import PartitionSpec as P

HIGHEST = lax.Precision.HIGHEST
STEP = 64
ROW_TILE = 128


def place_on(axis):
    return lax.axis_index(axis).astype(jnp.uint32)


def bit_of(axis, bit):
    return (place_on(axis) >> jnp.uint32(bit.bit_length() - 1)) & jnp.uint32(1)


def swap(value, axis, mask):
    pairs = [(index, index ^ mask) for index in range(lax.axis_size(axis))]
    return lax.ppermute(value, axis, pairs)


def bits_below(size):
    return [1 << place for place in range(size.bit_length() - 1)]


def half_of(value, which, dim):
    half = value.shape[dim] // 2
    return lax.dynamic_slice_in_dim(value, which * jnp.uint32(half), half, dim)


def reduce_half(value, axis, bit, dim):
    mine = bit_of(axis, bit)
    received = swap(half_of(value, mine ^ jnp.uint32(1), dim).astype(jnp.bfloat16), axis, bit)
    return half_of(value, mine, dim) + received.astype(jnp.float32)


def gather_half(value, axis, bit):
    mine = bit_of(axis, bit)
    received = swap(value, axis, bit)
    low = jnp.where(mine == 0, value, received)
    high = jnp.where(mine == 0, received, value)
    return jnp.concatenate([low, high], axis=0)


def order_of(matrix):
    chips = bits_below(lax.axis_size("col"))
    core, chips = chips[:1], chips[1:]
    turn = matrix % max(len(chips), 1)
    chips = chips[turn:] + chips[:turn]
    steps = [("col", bit) for bit in core + chips]
    return steps + [("row", bit) for bit in bits_below(lax.axis_size("row"))]


def tree_sum(parts):
    while len(parts) > 1:
        parts = [parts[i] + parts[i + 1] for i in range(0, len(parts), 2)]
    return parts[0]


def inverse_factor_kernel(gram_ref, inverse_ref, work_ref):
    count, rank, _ = gram_ref.shape
    step = min(STEP, rank)
    row = lax.broadcasted_iota(jnp.int32, (step, 2 * step), 0)
    lane = lax.broadcasted_iota(jnp.int32, (step, 2 * step), 1)
    eye = jnp.where(lane == row + step, 1.0, 0.0)[:, step:]
    full = lax.broadcasted_iota(jnp.int32, (step, rank), 1)
    for m in range(count):
        work_ref[m] = gram_ref[m]
    for start in range(0, rank, step):
        stop = start + step
        blocks = [
            jnp.concatenate([work_ref[m, start:stop, start:stop], eye], axis=1)
            for m in range(count)
        ]
        for j in range(step):
            for m in range(count):
                block = blocks[m]
                column = jnp.broadcast_to(block[:, j : j + 1], block.shape)
                pivot_row = block[j : j + 1, :] / column[j : j + 1, :]
                blocks[m] = block - jnp.where(row > j, column, 0.0) * pivot_row
        for m in range(count):
            block = blocks[m]
            diagonal = jnp.sum(jnp.where(lane == row, block, 0.0), axis=1, keepdims=True)
            inverse = block[:, step:] * lax.rsqrt(diagonal)
            unit = [jnp.zeros((step, start), jnp.float32)] if start else []
            unit += [eye]
            unit += [jnp.zeros((step, rank - stop), jnp.float32)] if stop < rank else []
            unit = jnp.concatenate(unit, axis=1) if len(unit) > 1 else unit[0]
            panel = jnp.where((full >= start) & (full < stop), unit, work_ref[m, start:stop, :])
            solved = jnp.dot(inverse, panel, precision=HIGHEST, preferred_element_type=jnp.float32)
            inverse_ref[m, start:stop, :] = jnp.where(full < stop, solved, 0.0)
            if stop < rank:
                rest = work_ref[m, stop:, :]
                wide = lax.broadcasted_iota(jnp.int32, rest.shape, 1)
                rest = jnp.where((wide >= start) & (wide < stop), 0.0, rest)
                work_ref[m, stop:, :] = rest - lax.dot_general(
                    solved[:, stop:],
                    solved,
                    (((0,), (0,)), ((), ())),
                    precision=HIGHEST,
                    preferred_element_type=jnp.float32,
                )


def inverse_factor(gram):
    return pl.pallas_call(
        inverse_factor_kernel,
        out_shape=jax.ShapeDtypeStruct(gram.shape, jnp.float32),
        scratch_shapes=[pltpu.VMEM(gram.shape, jnp.float32)],
        name="inverse_factor",
    )(gram)


def sum_everywhere(gram):
    columns = lax.axis_size("col")
    rows = lax.axis_size("row")
    chips = columns // 2
    mine = bit_of("col", 1)
    chip = place_on("col") >> jnp.uint32(1)
    value = half_of(gram, mine, 1) + swap(half_of(gram, mine ^ jnp.uint32(1), 1), "col", 1)
    chunk = value.shape[1] // chips

    def part(owner):
        return lax.dynamic_slice_in_dim(value, owner * jnp.uint32(chunk), chunk, 1)

    parts = [part(chip)]
    for mask in range(1, chips):
        parts.append(swap(part(chip ^ jnp.uint32(mask)), "col", 2 * mask))
    value = tree_sum(parts)
    value = tree_sum([value] + [swap(value, "row", mask) for mask in range(1, rows)])
    whole = jnp.zeros((value.shape[0], chunk * chips, value.shape[2]), jnp.float32)
    for mask in range(chips):
        piece = swap(value, "col", 2 * mask) if mask else value
        whole = lax.dynamic_update_slice_in_dim(whole, piece, (chip ^ jnp.uint32(mask)) * jnp.uint32(chunk), 1)
    other = swap(whole, "col", 1)
    low = jnp.where(mine == 0, whole, other)
    high = jnp.where(mine == 0, other, whole)
    return jnp.concatenate([low, high], axis=1)


def orthonormal(panels):
    grams = jnp.stack(
        [
            lax.dot_general(
                panel, panel, (((0,), (0,)), ((), ())), precision=HIGHEST, preferred_element_type=jnp.float32
            )
            for panel in panels
        ]
    )
    inverses = inverse_factor(sum_everywhere(grams))
    return [
        lax.dot_general(
            panel, inverses[m], (((1,), (1,)), ((), ())), precision=HIGHEST, preferred_element_type=jnp.float32
        )
        for m, panel in enumerate(panels)
    ]


def difference_kernel(adjusted_ref, base_ref, delta_ref):
    wide = adjusted_ref[...].astype(jnp.float32) - base_ref[...].astype(jnp.float32)
    delta_ref[...] = wide.astype(jnp.bfloat16)


def difference(adjusted, base, matrix):
    _, rows, width = base.shape
    tile = min(ROW_TILE, rows)
    stacked = pl.BlockSpec((None, tile, width), lambda i: (matrix, i, 0))
    return pl.pallas_call(
        difference_kernel,
        out_shape=jax.ShapeDtypeStruct((rows, width), jnp.bfloat16),
        grid=(pl.cdiv(rows, tile),),
        in_specs=[stacked, stacked],
        out_specs=pl.BlockSpec((tile, width), lambda i: (i, 0)),
        name="difference",
    )(adjusted, base)


def forward(delta, right):
    return jnp.dot(delta, right, preferred_element_type=jnp.float32)


def backward(delta, basis):
    return lax.dot_general(
        delta, basis, (((0,), (0,)), ((), ())), preferred_element_type=jnp.float32
    )


def all_columns(delta, basis, matrix):
    total = backward(delta, basis.astype(jnp.bfloat16))
    steps = order_of(matrix)
    for axis, bit in steps:
        total = reduce_half(total, axis, bit, 0)
    value = total.astype(jnp.bfloat16)
    for axis, bit in reversed(steps):
        value = gather_half(value, axis, bit)
    return value


def own_down(delta, basis, matrix):
    columns = lax.axis_size("col")
    rows = lax.axis_size("row")
    rank = basis.shape[1]
    places = bits_below(rows)
    parts = basis.reshape((basis.shape[0],) + (2,) * len(places) + (rank // rows,))
    parts = parts.transpose((0,) + tuple(range(len(places), 0, -1)) + (len(places) + 1,))
    total = backward(delta, parts.reshape(basis.shape).astype(jnp.bfloat16))
    bits = bits_below(columns)
    total = total.reshape((2,) * len(bits) + (-1, rank))
    left = list(reversed(bits))
    for axis, bit in order_of(matrix):
        if axis == "col":
            dim = left.index(bit)
            left.pop(dim)
            total = reduce_half(total, axis, bit, dim)
            total = lax.squeeze(total, (dim,))
        else:
            total = reduce_half(total, axis, bit, 1)
    return total


def local(base_flat, adjusted_flat, omega):
    matrices = base_flat.shape[0]
    hidden_units = base_flat.shape[1] * lax.axis_size("row") * lax.axis_size("col")
    every = range(matrices)
    deltas = [difference(adjusted_flat, base_flat, m) for m in every]
    whole_omega = lax.all_gather(omega, "col", axis=1, tiled=True)
    first = orthonormal([forward(deltas[m], whole_omega[m]) for m in every])
    columns = [all_columns(deltas[m], first[m], m) for m in every]
    last = orthonormal([forward(deltas[m], columns[m]) for m in every])
    down = jnp.stack([own_down(deltas[m], last[m], m) for m in every])
    up = jnp.stack([math.sqrt(hidden_units) * last[m] for m in every])
    return (up, down)


def solution(mesh):
    in_specs = (P(None, ("row", "col"), None), P(None, ("row", "col"), None), P(None, "col", None))
    out_specs = (P(None, ("row", "col"), None), P(None, "col", "row"))
    return jax.shard_map(local, mesh=mesh, in_specs=in_specs, out_specs=out_specs, check_vma=False)
```

```python
import functools
import math

import jax
import jax.numpy as jnp
from jax import lax
from jax.experimental import pallas as pl
from jax.experimental.pallas import tpu as pltpu
from jax.sharding import PartitionSpec as P

HIGHEST = lax.Precision.HIGHEST
STEP = 64
ROW_TILE = 64
WIDTH_TILE = 2048


def place_on(axis):
    return lax.axis_index(axis).astype(jnp.uint32)


def bit_of(axis, bit):
    return (place_on(axis) >> jnp.uint32(bit.bit_length() - 1)) & jnp.uint32(1)


def swap(value, axis, mask):
    pairs = [(index, index ^ mask) for index in range(lax.axis_size(axis))]
    return lax.ppermute(value, axis, pairs)


def bits_below(size):
    return [1 << place for place in range(size.bit_length() - 1)]


def half_of(value, which, dim):
    half = value.shape[dim] // 2
    return lax.dynamic_slice_in_dim(value, which * jnp.uint32(half), half, dim)


def reduce_half(value, axis, bit, dim):
    mine = bit_of(axis, bit)
    received = swap(half_of(value, mine ^ jnp.uint32(1), dim).astype(jnp.bfloat16), axis, bit)
    return half_of(value, mine, dim) + received.astype(jnp.float32)


def gather_half(value, axis, bit, dim):
    mine = bit_of(axis, bit)
    received = swap(value, axis, bit)
    low = jnp.where(mine == 0, value, received)
    high = jnp.where(mine == 0, received, value)
    return jnp.concatenate([low, high], axis=dim)


def arrange(parts, place):
    for bit in bits_below(len(parts)):
        odd = (place & jnp.uint32(bit)) != 0
        fresh = list(parts)
        for i in range(len(parts)):
            if not i & bit:
                fresh[i] = jnp.where(odd, parts[i | bit], parts[i])
                fresh[i | bit] = jnp.where(odd, parts[i], parts[i | bit])
        parts = fresh
    return parts


def chip_bits():
    return bits_below(lax.axis_size("col"))[1:]


def reduce_rows(value, dim):
    rows = lax.axis_size("row")
    place = place_on("row")
    size = value.shape[dim] // rows

    def part(owner):
        return lax.dynamic_slice_in_dim(value, owner * jnp.uint32(size), size, dim)

    total = [part(place)]
    for mask in range(1, rows):
        sent = part(place ^ jnp.uint32(mask)).astype(jnp.bfloat16)
        total.append(swap(sent, "row", mask).astype(jnp.float32))
    return tree_sum(total)


def gather_rows(value, dim):
    rows = lax.axis_size("row")
    parts = [value] + [swap(value, "row", mask) for mask in range(1, rows)]
    return jnp.concatenate(arrange(parts, place_on("row")), axis=dim)


def tree_sum(parts):
    while len(parts) > 1:
        parts = [parts[i] + parts[i + 1] for i in range(0, len(parts), 2)]
    return parts[0]


def inverse_factor_kernel(gram_ref, inverse_ref, work_ref):
    count, rank, _ = gram_ref.shape
    step = min(STEP, rank)
    row = lax.broadcasted_iota(jnp.int32, (step, 2 * step), 0)
    lane = lax.broadcasted_iota(jnp.int32, (step, 2 * step), 1)
    eye = jnp.where(lane == row + step, 1.0, 0.0)[:, step:]
    full = lax.broadcasted_iota(jnp.int32, (step, rank), 1)
    for m in range(count):
        work_ref[m] = gram_ref[m]
    for start in range(0, rank, step):
        stop = start + step
        blocks = [
            jnp.concatenate([work_ref[m, start:stop, start:stop], eye], axis=1)
            for m in range(count)
        ]
        for j in range(0, step, 2):
            for m in range(count):
                block = blocks[m]
                first = jnp.broadcast_to(block[:, j : j + 1], block.shape)
                second = jnp.broadcast_to(block[:, j + 1 : j + 2], block.shape)
                first_scale = 1.0 / first[j : j + 1, :]
                cross = first[j + 1 : j + 2, :]
                ratio = cross * first_scale
                top = block[j : j + 1, :]
                bottom = block[j + 1 : j + 2, :] - ratio * top
                second_scale = 1.0 / (second[j + 1 : j + 2, :] - cross * ratio)
                second = second - first * ratio
                blocks[m] = (
                    block
                    - jnp.where(row > j, first, 0.0) * (top * first_scale)
                    - jnp.where(row > j + 1, second, 0.0) * (bottom * second_scale)
                )
        for m in range(count):
            block = blocks[m]
            diagonal = jnp.sum(jnp.where(lane == row, block, 0.0), axis=1, keepdims=True)
            inverse = block[:, step:] * lax.rsqrt(diagonal)
            unit = [jnp.zeros((step, start), jnp.float32)] if start else []
            unit += [eye]
            unit += [jnp.zeros((step, rank - stop), jnp.float32)] if stop < rank else []
            unit = jnp.concatenate(unit, axis=1) if len(unit) > 1 else unit[0]
            panel = jnp.where((full >= start) & (full < stop), unit, work_ref[m, start:stop, :])
            solved = jnp.dot(inverse, panel, precision=HIGHEST, preferred_element_type=jnp.float32)
            inverse_ref[m, start:stop, :] = jnp.where(full < stop, solved, 0.0)
            if stop < rank:
                rest = work_ref[m, stop:, :]
                wide = lax.broadcasted_iota(jnp.int32, rest.shape, 1)
                rest = jnp.where((wide >= start) & (wide < stop), 0.0, rest)
                work_ref[m, stop:, :] = rest - lax.dot_general(
                    solved[:, stop:],
                    solved,
                    (((0,), (0,)), ((), ())),
                    precision=HIGHEST,
                    preferred_element_type=jnp.float32,
                )


def inverse_factor(gram):
    return pl.pallas_call(
        inverse_factor_kernel,
        out_shape=jax.ShapeDtypeStruct(gram.shape, jnp.float32),
        scratch_shapes=[pltpu.VMEM(gram.shape, jnp.float32)],
        name="inverse_factor",
    )(gram)


def sum_everywhere(gram):
    columns = lax.axis_size("col")
    rows = lax.axis_size("row")
    chips = columns // 2
    mine = bit_of("col", 1)
    chip = place_on("col") >> jnp.uint32(1)
    value = half_of(gram, mine, 1) + swap(half_of(gram, mine ^ jnp.uint32(1), 1), "col", 1)
    chunk = value.shape[1] // chips

    def part(owner):
        return lax.dynamic_slice_in_dim(value, owner * jnp.uint32(chunk), chunk, 1)

    parts = [part(chip)]
    for mask in range(1, chips):
        parts.append(swap(part(chip ^ jnp.uint32(mask)), "col", 2 * mask))
    value = tree_sum(parts)
    value = tree_sum([value] + [swap(value, "row", mask) for mask in range(1, rows)])
    parts = [value] + [swap(value, "col", 2 * mask) for mask in range(1, chips)]
    whole = jnp.concatenate(arrange(parts, chip), axis=1)
    return gather_half(whole, "col", 1, 1)


def product(left, right, dims):
    dims = ((dims[:1], dims[1:]), ((), ()))
    return lax.dot_general(left, right, dims, precision=HIGHEST, preferred_element_type=jnp.float32)


def factors(panels):
    grams = jnp.stack([product(panel, panel, (0, 0)) for panel in panels])
    return inverse_factor(sum_everywhere(grams))


def difference_kernel(adjusted_ref, base_ref, *delta_refs):
    wide = adjusted_ref[...].astype(jnp.float32) - base_ref[...].astype(jnp.float32)
    wide = jnp.swapaxes(wide, 0, 1)
    for m, delta_ref in enumerate(delta_refs):
        delta_ref[...] = wide[m].astype(jnp.bfloat16)


def differences(adjusted, base):
    matrices, rows, width = base.shape
    tall, wide = min(ROW_TILE, rows), min(WIDTH_TILE, width)
    stacked = pl.BlockSpec((tall, matrices, wide), lambda i, j: (i, 0, j))
    return pl.pallas_call(
        difference_kernel,
        out_shape=(jax.ShapeDtypeStruct((rows, width), jnp.bfloat16),) * matrices,
        grid=(pl.cdiv(rows, tall), pl.cdiv(width, wide)),
        in_specs=[stacked, stacked],
        out_specs=(pl.BlockSpec((tall, wide), lambda i, j: (i, j)),) * matrices,
        name="difference",
    )(adjusted.transpose(1, 0, 2), base.transpose(1, 0, 2))


def forward(delta, right):
    return jnp.dot(delta, right, preferred_element_type=jnp.float32)


def backward_kernel(basis_ref, delta_ref, out_ref):
    out_ref[...] = jnp.dot(basis_ref[...], delta_ref[...], preferred_element_type=jnp.float32)


def backward(delta, basis):
    rank, rows = basis.shape
    blocks = lax.axis_size("col")
    width = delta.shape[1] // blocks
    return pl.pallas_call(
        backward_kernel,
        out_shape=jax.ShapeDtypeStruct((2, blocks // 2, rank, width), jnp.float32),
        grid=(blocks,),
        in_specs=[
            pl.BlockSpec((rank, rows), lambda j: (0, 0)),
            pl.BlockSpec((rows, width), lambda j: (0, j)),
        ],
        out_specs=pl.BlockSpec((None, None, rank, width), lambda j: (j % 2, j // 2, 0, 0)),
        name="backward",
    )(basis, delta)


def all_columns(delta, basis):
    total = lax.dot_general(delta, basis, (((0,), (0,)), ((), ())), preferred_element_type=jnp.float32)
    chips = chip_bits()
    total = reduce_half(total, "col", 1, 0)
    half = total.shape[0] // 2
    shares = []
    for share, order in ((total[:half], chips), (total[half:], chips[::-1])):
        for bit in order:
            share = reduce_half(share, "col", bit, 0)
        shares.append(share)
    value = gather_rows(reduce_rows(jnp.stack(shares), 1).astype(jnp.bfloat16), 1)
    shares = []
    for index, order in ((0, chips[::-1]), (1, chips)):
        share = value[index]
        for bit in order:
            share = gather_half(share, "col", bit, 0)
        shares.append(share)
    return gather_half(jnp.concatenate(shares, axis=0), "col", 1, 0)


def own_down(delta, basis):
    rows = lax.axis_size("row")
    rank = basis.shape[0]
    bits = chip_bits()
    total = lax.squeeze(reduce_half(backward(delta, basis), "col", 1, 0), (0,))
    width = total.shape[2]
    part = rank // rows // 2
    total = total.reshape((2,) * len(bits) + (rows, 2, part, width))
    shares = []
    for index, order in ((0, bits), (1, bits[::-1])):
        share = lax.index_in_dim(total, index, len(bits) + 1, keepdims=False)
        left = bits[::-1]
        for bit in order:
            dim = left.index(bit)
            left.pop(dim)
            share = lax.squeeze(reduce_half(share, "col", bit, dim), (dim,))
        shares.append(share)
    return reduce_rows(jnp.concatenate(shares, axis=1), 0).reshape(rank // rows, width)


def local(base_flat, adjusted_flat, omega):
    matrices, _, rank = omega.shape
    hidden_units = base_flat.shape[1] * lax.axis_size("row") * lax.axis_size("col")
    every = range(matrices)
    deltas = differences(adjusted_flat, base_flat)
    whole_omega = lax.all_gather(omega, "col", axis=1, tiled=True)
    panels = [forward(deltas[m], whole_omega[m]) for m in every]
    inverses = factors(panels)
    first = [product(panels[m], inverses[m], (1, 1)).astype(jnp.bfloat16) for m in every]
    columns = [all_columns(deltas[m], first[m]) for m in every]
    panels = [forward(deltas[m], columns[m]) for m in every]
    inverses = factors(panels)
    last = [product(inverses[m], panels[m], (1, 1)).astype(jnp.bfloat16) for m in every]
    down = jnp.stack([own_down(deltas[m], last[m]) for m in every]).transpose(0, 2, 1)
    up = jnp.stack([math.sqrt(hidden_units) * product(panels[m], inverses[m], (1, 1)) for m in every])
    return (up, down)


def solution(mesh):
    in_specs = (P(None, ("row", "col"), None), P(None, ("row", "col"), None), P(None, "col", None))
    out_specs = (P(None, ("row", "col"), None), P(None, "col", "row"))
    return jax.shard_map(local, mesh=mesh, in_specs=in_specs, out_specs=out_specs, check_vma=False)
```

```python
import math

import jax
import jax.numpy as jnp
from jax import lax
from jax.experimental import pallas as pl
from jax.experimental.pallas import tpu as pltpu
from jax.sharding import PartitionSpec as P

HIGHEST = lax.Precision.HIGHEST
STEP = 64
PIVOTS = 4
ROW_TILE = 104
COLUMN_TILE = 1024


def place_on(axis):
    return lax.axis_index(axis).astype(jnp.uint32)


def bit_of(axis, bit):
    return (place_on(axis) >> jnp.uint32(bit.bit_length() - 1)) & jnp.uint32(1)


def swap(value, axis, mask):
    pairs = [(index, index ^ mask) for index in range(lax.axis_size(axis))]
    return lax.ppermute(value, axis, pairs)


def bits_below(size):
    return [1 << place for place in range(size.bit_length() - 1)]


def half_of(value, which, dim):
    half = value.shape[dim] // 2
    return lax.dynamic_slice_in_dim(value, which * jnp.uint32(half), half, dim)


def reduce_half(value, axis, bit, dim):
    mine = bit_of(axis, bit)
    received = swap(half_of(value, mine ^ jnp.uint32(1), dim).astype(jnp.bfloat16), axis, bit)
    return half_of(value, mine, dim) + received.astype(jnp.float32)


def gather_half(value, axis, bit, dim):
    mine = bit_of(axis, bit)
    received = swap(value, axis, bit)
    low = jnp.where(mine == 0, value, received)
    high = jnp.where(mine == 0, received, value)
    return jnp.concatenate([low, high], axis=dim)


def arrange(parts, place):
    for bit in bits_below(len(parts)):
        odd = (place & jnp.uint32(bit)) != 0
        fresh = list(parts)
        for i in range(len(parts)):
            if not i & bit:
                fresh[i] = jnp.where(odd, parts[i | bit], parts[i])
                fresh[i | bit] = jnp.where(odd, parts[i], parts[i | bit])
        parts = fresh
    return parts


def chip_bits():
    return bits_below(lax.axis_size("col"))[1:]


def reduce_rows(value, dim):
    rows = lax.axis_size("row")
    place = place_on("row")
    size = value.shape[dim] // rows

    def part(owner):
        return lax.dynamic_slice_in_dim(value, owner * jnp.uint32(size), size, dim)

    total = [part(place)]
    for mask in range(1, rows):
        sent = part(place ^ jnp.uint32(mask)).astype(jnp.bfloat16)
        total.append(swap(sent, "row", mask).astype(jnp.float32))
    return tree_sum(total)


def gather_rows(value, dim):
    rows = lax.axis_size("row")
    parts = [value] + [swap(value, "row", mask) for mask in range(1, rows)]
    return jnp.concatenate(arrange(parts, place_on("row")), axis=dim)


def tree_sum(parts):
    while len(parts) > 1:
        parts = [parts[i] + parts[i + 1] for i in range(0, len(parts), 2)]
    return parts[0]


def eliminate(block, row, j):
    columns = [jnp.broadcast_to(block[:, j + i : j + i + 1], block.shape) for i in range(PIVOTS)]
    rows = [block[j + i : j + i + 1, :] for i in range(PIVOTS)]
    corner = [[columns[k][j + i : j + i + 1, :] for k in range(PIVOTS)] for i in range(PIVOTS)]
    for i in range(PIVOTS):
        scale = 1.0 / corner[i][i]
        block = block - jnp.where(row > j + i, columns[i], 0.0) * (rows[i] * scale)
        for k in range(i + 1, PIVOTS):
            ratio = corner[k][i] * scale
            rows[k] = rows[k] - ratio * rows[i]
            columns[k] = columns[k] - columns[i] * ratio
            for l in range(k, PIVOTS):
                corner[l][k] = corner[l][k] - corner[l][i] * ratio
    return block


def inverse_factor_kernel(gram_ref, inverse_ref, work_ref):
    count, rank, _ = gram_ref.shape
    step = min(STEP, rank)
    row = lax.broadcasted_iota(jnp.int32, (step, 2 * step), 0)
    lane = lax.broadcasted_iota(jnp.int32, (step, 2 * step), 1)
    eye = jnp.where(lane == row + step, 1.0, 0.0)[:, step:]
    full = lax.broadcasted_iota(jnp.int32, (step, rank), 1)
    for m in range(count):
        work_ref[m] = gram_ref[m]
    for start in range(0, rank, step):
        stop = start + step
        blocks = [
            jnp.concatenate([work_ref[m, start:stop, start:stop], eye], axis=1)
            for m in range(count)
        ]
        for j in range(0, step, PIVOTS):
            for m in range(count):
                blocks[m] = eliminate(blocks[m], row, j)
        for m in range(count):
            block = blocks[m]
            diagonal = jnp.sum(jnp.where(lane == row, block, 0.0), axis=1, keepdims=True)
            inverse = block[:, step:] * lax.rsqrt(diagonal)
            unit = [jnp.zeros((step, start), jnp.float32)] if start else []
            unit += [eye]
            unit += [jnp.zeros((step, rank - stop), jnp.float32)] if stop < rank else []
            unit = jnp.concatenate(unit, axis=1) if len(unit) > 1 else unit[0]
            panel = jnp.where((full >= start) & (full < stop), unit, work_ref[m, start:stop, :])
            solved = jnp.dot(inverse, panel, precision=HIGHEST, preferred_element_type=jnp.float32)
            inverse_ref[m, start:stop, :] = jnp.where(full < stop, solved, 0.0)
            if stop < rank:
                rest = work_ref[m, stop:, :]
                wide = lax.broadcasted_iota(jnp.int32, rest.shape, 1)
                rest = jnp.where((wide >= start) & (wide < stop), 0.0, rest)
                work_ref[m, stop:, :] = rest - lax.dot_general(
                    solved[:, stop:],
                    solved,
                    (((0,), (0,)), ((), ())),
                    precision=HIGHEST,
                    preferred_element_type=jnp.float32,
                )


def inverse_factor(gram):
    return pl.pallas_call(
        inverse_factor_kernel,
        out_shape=jax.ShapeDtypeStruct(gram.shape, jnp.float32),
        scratch_shapes=[pltpu.VMEM(gram.shape, jnp.float32)],
        name="inverse_factor",
    )(gram)


def sum_everywhere(gram):
    columns = lax.axis_size("col")
    rows = lax.axis_size("row")
    chips = columns // 2
    mine = bit_of("col", 1)
    chip = place_on("col") >> jnp.uint32(1)
    value = half_of(gram, mine, 1) + swap(half_of(gram, mine ^ jnp.uint32(1), 1), "col", 1)
    chunk = value.shape[1] // chips

    def part(owner):
        return lax.dynamic_slice_in_dim(value, owner * jnp.uint32(chunk), chunk, 1)

    parts = [part(chip)]
    for mask in range(1, chips):
        parts.append(swap(part(chip ^ jnp.uint32(mask)), "col", 2 * mask))
    value = tree_sum(parts)
    value = tree_sum([value] + [swap(value, "row", mask) for mask in range(1, rows)])
    parts = [value] + [swap(value, "col", 2 * mask) for mask in range(1, chips)]
    whole = jnp.concatenate(arrange(parts, chip), axis=1)
    return gather_half(whole, "col", 1, 1)


def product(left, right, dims):
    dims = ((dims[:1], dims[1:]), ((), ()))
    return lax.dot_general(left, right, dims, precision=HIGHEST, preferred_element_type=jnp.float32)


def factors(panels):
    grams = jnp.stack([product(panel, panel, (0, 0)) for panel in panels])
    return inverse_factor(sum_everywhere(grams))


def difference_kernel(adjusted_ref, base_ref, *delta_refs):
    wide = adjusted_ref[...].astype(jnp.float32) - base_ref[...].astype(jnp.float32)
    wide = jnp.swapaxes(wide, 0, 1)
    for m, delta_ref in enumerate(delta_refs):
        delta_ref[...] = wide[m].astype(jnp.bfloat16)


def differences(adjusted, base):
    matrices, rows, width = base.shape
    tall = min(ROW_TILE, rows)
    stacked = pl.BlockSpec((tall, matrices, width), lambda i: (i, 0, 0))
    return pl.pallas_call(
        difference_kernel,
        out_shape=(jax.ShapeDtypeStruct((rows, width), jnp.bfloat16),) * matrices,
        grid=(pl.cdiv(rows, tall),),
        in_specs=[stacked, stacked],
        out_specs=(pl.BlockSpec((tall, width), lambda i: (i, 0)),) * matrices,
        name="difference",
    )(adjusted.transpose(1, 0, 2), base.transpose(1, 0, 2))


def forward_kernel(place_ref, delta_ref, *refs):
    part_refs, out_ref = refs[:-1], refs[-1]
    step = pl.program_id(0)
    width = delta_ref.shape[1]
    each = part_refs[0].shape[0] // width

    @pl.when(step == 0)
    def _():
        out_ref[...] = jnp.zeros_like(out_ref)

    for index, part_ref in enumerate(part_refs):

        @pl.when(step // each == index)
        def _(part_ref=part_ref):
            start = pl.multiple_of((step % each) * width, width)
            part = part_ref[pl.ds(start, width), :]
            out_ref[...] += jnp.dot(delta_ref[...], part, preferred_element_type=jnp.float32)


def forward(delta, parts, place):
    rows = delta.shape[0]
    length, rank = parts[0].shape
    width = min(length, COLUMN_TILE)
    each = length // width

    def column(step, place_ref):
        return (0, (place_ref[0] ^ (step // each)) * each + step % each)

    return pl.pallas_call(
        forward_kernel,
        out_shape=jax.ShapeDtypeStruct((rows, rank), jnp.float32),
        grid_spec=pltpu.PrefetchScalarGridSpec(
            num_scalar_prefetch=1,
            grid=(len(parts) * each,),
            in_specs=[pl.BlockSpec((rows, width), column)]
            + [pl.BlockSpec((length, rank), lambda step, place_ref: (0, 0))] * len(parts),
            out_specs=pl.BlockSpec((rows, rank), lambda step, place_ref: (0, 0)),
        ),
        name="forward",
        cost_estimate=pl.CostEstimate(
            flops=2 * rows * rank * delta.shape[1],
            transcendentals=0,
            bytes_accessed=2 * rows * delta.shape[1],
        ),
    )(place[None], delta, *parts)


def backward(delta, basis):
    return lax.dot_general(delta, basis, (((0,), (0,)), ((), ())), preferred_element_type=jnp.float32)


def near_parts(share):
    return [share] + [swap(share, "col", mask) for mask in range(2, lax.axis_size("col"), 2)]


def with_other_core(near):
    parts = []
    for part in near:
        parts += [part, swap(part, "col", 1)]
    return parts


def all_columns(delta, basis):
    chips = chip_bits()
    total = reduce_half(backward(delta, basis), "col", 1, 0)
    half = total.shape[0] // 2
    shares = []
    for share, order in ((total[:half], chips), (total[half:], chips[::-1])):
        for bit in order:
            share = reduce_half(share, "col", bit, 0)
        shares.append(share)
    value = gather_rows(reduce_rows(jnp.stack(shares), 1).astype(jnp.bfloat16), 1)
    shares = []
    for index, order in ((0, chips[::-1]), (1, chips)):
        share = value[index]
        for bit in order:
            share = gather_half(share, "col", bit, 0)
        shares.append(share)
    half = jnp.concatenate(shares, axis=0)
    return [half, swap(half, "col", 1)]


def transposed_kernel(*refs):
    out_ref, start = refs[-1], 0
    for ref in refs[:-1]:
        out_ref[:, start : start + ref.shape[0]] = ref[...].T
        start += ref.shape[0]


def transposed(pieces):
    length = sum(piece.shape[0] for piece in pieces)
    return pl.pallas_call(
        transposed_kernel,
        out_shape=jax.ShapeDtypeStruct((pieces[0].shape[1], length), jnp.float32),
        name="transposed",
    )(*pieces)


def own_down(delta, basis):
    bits = chip_bits()
    total = lax.optimization_barrier(backward(delta, basis))
    rank = total.shape[1]
    width = total.shape[0] // lax.axis_size("col")
    total = total.reshape((2,) * len(bits) + (2, width, rank))
    total = lax.squeeze(reduce_half(total, "col", 1, len(bits)), (len(bits),))
    shares = []
    for start, order in ((0, bits), (width // 2, bits[::-1])):
        share = lax.slice_in_dim(total, start, start + width // 2, axis=len(bits))
        left = bits[::-1]
        for bit in order:
            dim = left.index(bit)
            left.pop(dim)
            share = lax.squeeze(reduce_half(share, "col", bit, dim), (dim,))
        shares.append(share)
    return reduce_rows(transposed(shares), 0)


def local(base_flat, adjusted_flat, omega):
    matrices, _, rank = omega.shape
    hidden_units = base_flat.shape[1] * lax.axis_size("row") * lax.axis_size("col")
    every = range(matrices)
    near = [near_parts(omega[m]) for m in every]
    deltas = differences(adjusted_flat, base_flat)
    for m in every:
        gated, near[m] = lax.optimization_barrier((deltas, near[m]))
        deltas = deltas if m else gated
    place = lax.axis_index("col")
    core = place & 1
    panels = [forward(deltas[m], with_other_core(near[m]), place) for m in every]
    inverses = factors(panels)
    first = [product(panels[m], inverses[m], (1, 1)).astype(jnp.bfloat16) for m in every]
    columns = [all_columns(deltas[m], first[m]) for m in every]
    panels = [forward(deltas[m], columns[m], core) for m in every]
    inverses = factors(panels)
    last = [product(panels[m], inverses[m], (1, 1)) for m in every]
    down = jnp.stack([own_down(deltas[m], last[m].astype(jnp.bfloat16)) for m in every]).transpose(0, 2, 1)
    up = jnp.stack([math.sqrt(hidden_units) * last[m] for m in every])
    return (up, down)


def solution(mesh):
    in_specs = (P(None, ("row", "col"), None), P(None, ("row", "col"), None), P(None, "col", None))
    out_specs = (P(None, ("row", "col"), None), P(None, "col", "row"))
    return jax.shard_map(local, mesh=mesh, in_specs=in_specs, out_specs=out_specs, check_vma=False)
```

```python
import math

import jax
import jax.numpy as jnp
from jax import lax
from jax.experimental import pallas as pl
from jax.experimental.pallas import tpu as pltpu
from jax.sharding import PartitionSpec as P

HIGHEST = lax.Precision.HIGHEST
STEP = 64
PIVOTS = 4
ROW_TILE = 104


def place_on(axis):
    return lax.axis_index(axis).astype(jnp.uint32)


def bit_of(axis, bit):
    return (place_on(axis) >> jnp.uint32(bit.bit_length() - 1)) & jnp.uint32(1)


def swap(value, axis, mask):
    pairs = [(index, index ^ mask) for index in range(lax.axis_size(axis))]
    return lax.ppermute(value, axis, pairs)


def bits_below(size):
    return [1 << place for place in range(size.bit_length() - 1)]


def half_of(value, which, dim):
    half = value.shape[dim] // 2
    return lax.dynamic_slice_in_dim(value, which * jnp.uint32(half), half, dim)


def reduce_half(value, axis, bit, dim):
    mine = bit_of(axis, bit)
    received = swap(half_of(value, mine ^ jnp.uint32(1), dim).astype(jnp.bfloat16), axis, bit)
    return half_of(value, mine, dim) + received.astype(jnp.float32)


def gather_half(value, axis, bit, dim):
    mine = bit_of(axis, bit)
    received = swap(value, axis, bit)
    low = jnp.where(mine == 0, value, received)
    high = jnp.where(mine == 0, received, value)
    return jnp.concatenate([low, high], axis=dim)


def arrange(parts, place):
    for bit in bits_below(len(parts)):
        odd = (place & jnp.uint32(bit)) != 0
        fresh = list(parts)
        for i in range(len(parts)):
            if not i & bit:
                fresh[i] = jnp.where(odd, parts[i | bit], parts[i])
                fresh[i | bit] = jnp.where(odd, parts[i], parts[i | bit])
        parts = fresh
    return parts


def chip_bits():
    return bits_below(lax.axis_size("col"))[1:]


def reduce_rows(value, dim):
    rows = lax.axis_size("row")
    place = place_on("row")
    size = value.shape[dim] // rows

    def part(owner):
        return lax.dynamic_slice_in_dim(value, owner * jnp.uint32(size), size, dim)

    total = [part(place)]
    for mask in range(1, rows):
        sent = part(place ^ jnp.uint32(mask)).astype(jnp.bfloat16)
        total.append(swap(sent, "row", mask).astype(jnp.float32))
    return tree_sum(total)


def gather_rows(value, dim):
    rows = lax.axis_size("row")
    parts = [value] + [swap(value, "row", mask) for mask in range(1, rows)]
    return jnp.concatenate(arrange(parts, place_on("row")), axis=dim)


def tree_sum(parts):
    while len(parts) > 1:
        parts = [parts[i] + parts[i + 1] for i in range(0, len(parts), 2)]
    return parts[0]


def eliminate(block, row, j):
    columns = [jnp.broadcast_to(block[:, j + i : j + i + 1], block.shape) for i in range(PIVOTS)]
    rows = [block[j + i : j + i + 1, :] for i in range(PIVOTS)]
    corner = [[columns[k][j + i : j + i + 1, :] for k in range(PIVOTS)] for i in range(PIVOTS)]
    for i in range(PIVOTS):
        scale = 1.0 / corner[i][i]
        block = block - jnp.where(row > j + i, columns[i], 0.0) * (rows[i] * scale)
        for k in range(i + 1, PIVOTS):
            ratio = corner[k][i] * scale
            rows[k] = rows[k] - ratio * rows[i]
            columns[k] = columns[k] - columns[i] * ratio
            for l in range(k, PIVOTS):
                corner[l][k] = corner[l][k] - corner[l][i] * ratio
    return block


def inverse_factor_kernel(gram_ref, inverse_ref, work_ref):
    count, rank, _ = gram_ref.shape
    step = min(STEP, rank)
    row = lax.broadcasted_iota(jnp.int32, (step, 2 * step), 0)
    lane = lax.broadcasted_iota(jnp.int32, (step, 2 * step), 1)
    eye = jnp.where(lane == row + step, 1.0, 0.0)[:, step:]
    full = lax.broadcasted_iota(jnp.int32, (step, rank), 1)
    for m in range(count):
        work_ref[m] = gram_ref[m]
    for start in range(0, rank, step):
        stop = start + step
        blocks = [
            jnp.concatenate([work_ref[m, start:stop, start:stop], eye], axis=1)
            for m in range(count)
        ]
        for j in range(0, step, PIVOTS):
            for m in range(count):
                blocks[m] = eliminate(blocks[m], row, j)
        for m in range(count):
            block = blocks[m]
            diagonal = jnp.sum(jnp.where(lane == row, block, 0.0), axis=1, keepdims=True)
            inverse = block[:, step:] * lax.rsqrt(diagonal)
            unit = [jnp.zeros((step, start), jnp.float32)] if start else []
            unit += [eye]
            unit += [jnp.zeros((step, rank - stop), jnp.float32)] if stop < rank else []
            unit = jnp.concatenate(unit, axis=1) if len(unit) > 1 else unit[0]
            panel = jnp.where((full >= start) & (full < stop), unit, work_ref[m, start:stop, :])
            solved = jnp.dot(inverse, panel, precision=HIGHEST, preferred_element_type=jnp.float32)
            inverse_ref[m, start:stop, :] = jnp.where(full < stop, solved, 0.0)
            if stop < rank:
                rest = work_ref[m, stop:, :]
                wide = lax.broadcasted_iota(jnp.int32, rest.shape, 1)
                rest = jnp.where((wide >= start) & (wide < stop), 0.0, rest)
                work_ref[m, stop:, :] = rest - lax.dot_general(
                    solved[:, stop:],
                    solved,
                    (((0,), (0,)), ((), ())),
                    precision=HIGHEST,
                    preferred_element_type=jnp.float32,
                )


def inverse_factor(gram):
    return pl.pallas_call(
        inverse_factor_kernel,
        out_shape=jax.ShapeDtypeStruct(gram.shape, jnp.float32),
        scratch_shapes=[pltpu.VMEM(gram.shape, jnp.float32)],
        name="inverse_factor",
    )(gram)


def sum_everywhere(gram):
    columns = lax.axis_size("col")
    rows = lax.axis_size("row")
    chips = columns // 2
    mine = bit_of("col", 1)
    chip = place_on("col") >> jnp.uint32(1)
    value = half_of(gram, mine, 1) + swap(half_of(gram, mine ^ jnp.uint32(1), 1), "col", 1)
    chunk = value.shape[1] // chips

    def part(owner):
        return lax.dynamic_slice_in_dim(value, owner * jnp.uint32(chunk), chunk, 1)

    parts = [part(chip)]
    for mask in range(1, chips):
        parts.append(swap(part(chip ^ jnp.uint32(mask)), "col", 2 * mask))
    value = tree_sum(parts)
    value = tree_sum([value] + [swap(value, "row", mask) for mask in range(1, rows)])
    parts = [value] + [swap(value, "col", 2 * mask) for mask in range(1, chips)]
    whole = jnp.concatenate(arrange(parts, chip), axis=1)
    return gather_half(whole, "col", 1, 1)


def product(left, right, dims):
    dims = ((dims[:1], dims[1:]), ((), ()))
    return lax.dot_general(left, right, dims, precision=HIGHEST, preferred_element_type=jnp.float32)


def factors(panels):
    grams = jnp.stack([product(panel, panel, (0, 0)) for panel in panels])
    return inverse_factor(sum_everywhere(grams))


def difference_kernel(adjusted_ref, base_ref, *delta_refs):
    wide = adjusted_ref[...].astype(jnp.float32) - base_ref[...].astype(jnp.float32)
    wide = jnp.swapaxes(wide, 0, 1)
    for m, delta_ref in enumerate(delta_refs):
        delta_ref[...] = wide[m].astype(jnp.bfloat16)


def differences(adjusted, base):
    matrices, rows, width = base.shape
    tall = min(ROW_TILE, rows)
    stacked = pl.BlockSpec((tall, matrices, width), lambda i: (i, 0, 0))
    return pl.pallas_call(
        difference_kernel,
        out_shape=(jax.ShapeDtypeStruct((rows, width), jnp.bfloat16),) * matrices,
        grid=(pl.cdiv(rows, tall),),
        in_specs=[stacked, stacked],
        out_specs=(pl.BlockSpec((tall, width), lambda i: (i, 0)),) * matrices,
        name="difference",
    )(adjusted.transpose(1, 0, 2), base.transpose(1, 0, 2))


def assemble_kernel(place_ref, *refs):
    *part_refs, out_ref, sems = refs
    length = part_refs[0].shape[0]
    copies = []
    for index, part_ref in enumerate(part_refs):
        start = pl.multiple_of((place_ref[0] ^ index) * length, length)
        copies.append(pltpu.make_async_copy(part_ref, out_ref.at[pl.ds(start, length), :], sems.at[index]))
    for copy in copies:
        copy.start()
    for copy in copies:
        copy.wait()


def assemble(parts, place):
    length, rank = parts[0].shape
    return pl.pallas_call(
        assemble_kernel,
        out_shape=jax.ShapeDtypeStruct((len(parts) * length, rank), parts[0].dtype),
        in_specs=[pl.BlockSpec(memory_space=pltpu.SMEM)]
        + [pl.BlockSpec(memory_space=pl.ANY)] * len(parts),
        out_specs=pl.BlockSpec(memory_space=pl.ANY),
        scratch_shapes=[pltpu.SemaphoreType.DMA((len(parts),))],
        name="assemble",
    )(place[None], *parts)


def forward(delta, right):
    return jnp.dot(delta, right, preferred_element_type=jnp.float32)


def backward(delta, basis):
    return lax.dot_general(delta, basis, (((0,), (0,)), ((), ())), preferred_element_type=jnp.float32)


def near_parts(share):
    return [share] + [swap(share, "col", mask) for mask in range(2, lax.axis_size("col"), 2)]


def with_other_core(near):
    parts = []
    for part in near:
        parts += [part, swap(part, "col", 1)]
    return parts


def reduce_chips(shares_of, leading):
    bits = chip_bits()

    def step(share, order, turn):
        if not leading:
            return reduce_half(share, "col", order[turn], 0)
        left = sorted(order[turn:], reverse=True)
        dim = left.index(order[turn])
        return lax.squeeze(reduce_half(share, "col", order[turn], dim), (dim,))

    orders = (bits, bits[::-1])
    for m, shares in enumerate(shares_of):
        for turn in range(len(bits)):
            shares = [step(share, order, turn) for share, order in zip(shares, orders)]
            if turn == 0 and m + 1 < len(shares_of):
                shares, shares_of[m + 1] = lax.optimization_barrier((shares, shares_of[m + 1]))
        shares_of[m] = shares
    return shares_of


def core_sum(delta, basis):
    bits = chip_bits()
    total = lax.optimization_barrier(backward(delta, basis))
    width = total.shape[0] // lax.axis_size("col")
    total = total.reshape((2,) * len(bits) + (2, width, total.shape[1]))
    return lax.squeeze(reduce_half(total, "col", 1, len(bits)), (len(bits),))


def two_shares(total, dim):
    half = total.shape[dim] // 2
    return [lax.slice_in_dim(total, start, start + half, axis=dim) for start in (0, half)]


def all_columns(deltas, bases):
    bits = chip_bits()
    totals = [reduce_half(backward(delta, basis), "col", 1, 0) for delta, basis in zip(deltas, bases)]
    columns = []
    for shares in reduce_chips([two_shares(total, 0) for total in totals], False):
        value = gather_rows(reduce_rows(jnp.stack(shares), 1).astype(jnp.bfloat16), 1)
        shares = []
        for index, order in ((0, bits[::-1]), (1, bits)):
            share = value[index]
            for bit in order:
                share = gather_half(share, "col", bit, 0)
            shares.append(share)
        columns.append(gather_half(jnp.concatenate(shares, axis=0), "col", 1, 0))
    return columns


def transposed_kernel(*refs):
    out_ref, start = refs[-1], 0
    for ref in refs[:-1]:
        out_ref[:, start : start + ref.shape[0]] = ref[...].T
        start += ref.shape[0]


def transposed(pieces):
    length = sum(piece.shape[0] for piece in pieces)
    return pl.pallas_call(
        transposed_kernel,
        out_shape=jax.ShapeDtypeStruct((pieces[0].shape[1], length), jnp.float32),
        name="transposed",
    )(*pieces)


def own_downs(deltas, bases):
    totals = [core_sum(delta, basis) for delta, basis in zip(deltas, bases)]
    shares_of = reduce_chips([two_shares(total, total.ndim - 2) for total in totals], True)
    return [reduce_rows(transposed(shares), 0) for shares in shares_of]


def local(base_flat, adjusted_flat, omega):
    matrices, _, rank = omega.shape
    hidden_units = base_flat.shape[1] * lax.axis_size("row") * lax.axis_size("col")
    every = range(matrices)
    near = [near_parts(omega[m]) for m in every]
    deltas = differences(adjusted_flat, base_flat)
    for m in every:
        gated, near[m] = lax.optimization_barrier((deltas, near[m]))
        deltas = deltas if m else gated
    place = lax.axis_index("col")
    panels = [forward(deltas[m], assemble(with_other_core(near[m]), place)) for m in every]
    inverses = factors(panels)
    first = [product(panels[m], inverses[m], (1, 1)).astype(jnp.bfloat16) for m in every]
    columns = all_columns(deltas, first)
    panels = [forward(deltas[m], columns[m]) for m in every]
    inverses = factors(panels)
    last = [product(panels[m], inverses[m], (1, 1)) for m in every]
    down = jnp.stack(own_downs(deltas, [basis.astype(jnp.bfloat16) for basis in last])).transpose(0, 2, 1)
    up = jnp.stack([math.sqrt(hidden_units) * last[m] for m in every])
    return (up, down)


def solution(mesh):
    in_specs = (P(None, ("row", "col"), None), P(None, ("row", "col"), None), P(None, "col", None))
    out_specs = (P(None, ("row", "col"), None), P(None, "col", "row"))
    return jax.shard_map(local, mesh=mesh, in_specs=in_specs, out_specs=out_specs, check_vma=False)
```

```python
import math

import jax
import jax.numpy as jnp
from jax import lax
from jax.experimental import pallas as pl
from jax.experimental.pallas import tpu as pltpu
from jax.sharding import PartitionSpec as P


HIGHEST = lax.Precision.HIGHEST
STEP = 64
SMALL_KERNEL_BYTES = 12 << 20
PIVOTS = 4
ROW_TILE = 104


def place_on(axis):
    return lax.axis_index(axis).astype(jnp.uint32)


def bit_of(axis, bit):
    return (place_on(axis) >> jnp.uint32(bit.bit_length() - 1)) & jnp.uint32(1)


def swap(value, axis, mask):
    pairs = [(index, index ^ mask) for index in range(lax.axis_size(axis))]
    return lax.ppermute(value, axis, pairs)


def bits_below(size):
    return [1 << place for place in range(size.bit_length() - 1)]


def half_of(value, which, dim):
    half = value.shape[dim] // 2
    return lax.dynamic_slice_in_dim(value, which * jnp.uint32(half), half, dim)


def reduce_half(value, axis, bit, dim):
    mine = bit_of(axis, bit)
    received = swap(half_of(value, mine ^ jnp.uint32(1), dim).astype(jnp.bfloat16), axis, bit)
    return half_of(value, mine, dim).astype(jnp.float32) + received.astype(jnp.float32)


def gather_half(value, axis, bit, dim):
    mine = bit_of(axis, bit)
    received = swap(value, axis, bit)
    low = jnp.where(mine == 0, value, received)
    high = jnp.where(mine == 0, received, value)
    return jnp.concatenate([low, high], axis=dim)


def arrange(parts, place):
    for bit in bits_below(len(parts)):
        odd = (place & jnp.uint32(bit)) != 0
        fresh = list(parts)
        for i in range(len(parts)):
            if not i & bit:
                fresh[i] = jnp.where(odd, parts[i | bit], parts[i])
                fresh[i | bit] = jnp.where(odd, parts[i], parts[i | bit])
        parts = fresh
    return parts


def chip_bits():
    return bits_below(lax.axis_size("col"))[1:]


def reduce_rows(value, dim):
    rows = lax.axis_size("row")
    place = place_on("row")
    size = value.shape[dim] // rows

    def part(owner):
        return lax.dynamic_slice_in_dim(value, owner * jnp.uint32(size), size, dim)

    total = [part(place)]
    for mask in range(1, rows):
        sent = part(place ^ jnp.uint32(mask)).astype(jnp.bfloat16)
        total.append(swap(sent, "row", mask).astype(jnp.float32))
    return tree_sum(total)


def gather_rows(value, dim):
    rows = lax.axis_size("row")
    parts = [value] + [swap(value, "row", mask) for mask in range(1, rows)]
    return jnp.concatenate(arrange(parts, place_on("row")), axis=dim)


def tree_sum(parts):
    while len(parts) > 1:
        parts = [parts[i] + parts[i + 1] for i in range(0, len(parts), 2)]
    return parts[0]


def eliminate(block, row, j):
    columns = [jnp.broadcast_to(block[:, j + i : j + i + 1], block.shape) for i in range(PIVOTS)]
    rows = [block[j + i : j + i + 1, :] for i in range(PIVOTS)]
    corner = [[columns[k][j + i : j + i + 1, :] for k in range(PIVOTS)] for i in range(PIVOTS)]
    for i in range(PIVOTS):
        scale = 1.0 / corner[i][i]
        block = block - jnp.where(row > j + i, columns[i], 0.0) * (rows[i] * scale)
        for k in range(i + 1, PIVOTS):
            ratio = corner[k][i] * scale
            rows[k] = rows[k] - ratio * rows[i]
            columns[k] = columns[k] - columns[i] * ratio
            for l in range(k, PIVOTS):
                corner[l][k] = corner[l][k] - corner[l][i] * ratio
    return block


def inverse_factor_kernel(gram_ref, inverse_ref, work_ref):
    count, rank, _ = gram_ref.shape
    step = min(STEP, rank)
    row = lax.broadcasted_iota(jnp.int32, (step, 2 * step), 0)
    lane = lax.broadcasted_iota(jnp.int32, (step, 2 * step), 1)
    eye = jnp.where(lane == row + step, 1.0, 0.0)[:, step:]
    full = lax.broadcasted_iota(jnp.int32, (step, rank), 1)
    for m in range(count):
        work_ref[m] = gram_ref[m]
    for start in range(0, rank, step):
        stop = start + step
        blocks = [
            jnp.concatenate([work_ref[m, start:stop, start:stop], eye], axis=1)
            for m in range(count)
        ]
        for j in range(0, step, PIVOTS):
            for m in range(count):
                blocks[m] = eliminate(blocks[m], row, j)
        for m in range(count):
            block = blocks[m]
            diagonal = jnp.sum(jnp.where(lane == row, block, 0.0), axis=1, keepdims=True)
            inverse = block[:, step:] * lax.rsqrt(diagonal)
            unit = [jnp.zeros((step, start), jnp.float32)] if start else []
            unit += [eye]
            unit += [jnp.zeros((step, rank - stop), jnp.float32)] if stop < rank else []
            unit = jnp.concatenate(unit, axis=1) if len(unit) > 1 else unit[0]
            panel = jnp.where((full >= start) & (full < stop), unit, work_ref[m, start:stop, :])
            solved = jnp.dot(inverse, panel, precision=HIGHEST, preferred_element_type=jnp.float32)
            inverse_ref[m, start:stop, :] = jnp.where(full < stop, solved, 0.0)
            if stop < rank:
                rest = work_ref[m, stop:, :]
                wide = lax.broadcasted_iota(jnp.int32, rest.shape, 1)
                rest = jnp.where((wide >= start) & (wide < stop), 0.0, rest)
                work_ref[m, stop:, :] = rest - lax.dot_general(
                    solved[:, stop:],
                    solved,
                    (((0,), (0,)), ((), ())),
                    precision=HIGHEST,
                    preferred_element_type=jnp.float32,
                )


def inverse_factor(gram):
    return pl.pallas_call(
        inverse_factor_kernel,
        out_shape=jax.ShapeDtypeStruct(gram.shape, jnp.float32),
        scratch_shapes=[pltpu.VMEM(gram.shape, jnp.float32)],
        compiler_params=pltpu.CompilerParams(vmem_limit_bytes=SMALL_KERNEL_BYTES),
        name="inverse_factor",
    )(gram)


def sum_everywhere(gram):
    columns = lax.axis_size("col")
    rows = lax.axis_size("row")
    chips = columns // 2
    mine = bit_of("col", 1)
    chip = place_on("col") >> jnp.uint32(1)
    value = half_of(gram, mine, 1) + swap(half_of(gram, mine ^ jnp.uint32(1), 1), "col", 1)
    chunk = value.shape[1] // chips

    def part(owner):
        return lax.dynamic_slice_in_dim(value, owner * jnp.uint32(chunk), chunk, 1)

    parts = [part(chip)]
    for mask in range(1, chips):
        parts.append(swap(part(chip ^ jnp.uint32(mask)), "col", 2 * mask))
    value = tree_sum(parts)
    value = tree_sum([value] + [swap(value, "row", mask) for mask in range(1, rows)])
    parts = [value] + [swap(value, "col", 2 * mask) for mask in range(1, chips)]
    whole = jnp.concatenate(arrange(parts, chip), axis=1)
    return gather_half(whole, "col", 1, 1)


def product(left, right, dims):
    dims = ((dims[:1], dims[1:]), ((), ()))
    return lax.dot_general(left, right, dims, precision=HIGHEST, preferred_element_type=jnp.float32)


def factors(panels):
    grams = jnp.stack([product(panel, panel, (0, 0)) for panel in panels])
    return inverse_factor(sum_everywhere(grams))


def difference_kernel(adjusted_ref, base_ref, *delta_refs):
    wide = adjusted_ref[...].astype(jnp.float32) - base_ref[...].astype(jnp.float32)
    wide = jnp.swapaxes(wide, 0, 1)
    for m, delta_ref in enumerate(delta_refs):
        delta_ref[...] = wide[m].astype(jnp.bfloat16)


def differences(adjusted, base):
    matrices, rows, width = base.shape
    tall = min(ROW_TILE, rows)
    stacked = pl.BlockSpec((tall, matrices, width), lambda i: (i, 0, 0))
    return pl.pallas_call(
        difference_kernel,
        out_shape=(jax.ShapeDtypeStruct((rows, width), jnp.bfloat16),) * matrices,
        grid=(pl.cdiv(rows, tall),),
        in_specs=[stacked, stacked],
        out_specs=(pl.BlockSpec((tall, width), lambda i: (i, 0)),) * matrices,
        name="difference",
    )(adjusted.transpose(1, 0, 2), base.transpose(1, 0, 2))


def assemble_kernel(place_ref, *refs):
    *part_refs, out_ref, sems = refs
    length = part_refs[0].shape[0]
    copies = []
    for index, part_ref in enumerate(part_refs):
        start = pl.multiple_of((place_ref[0] ^ index) * length, length)
        copies.append(pltpu.make_async_copy(part_ref, out_ref.at[pl.ds(start, length), :], sems.at[index]))
    for copy in copies:
        copy.start()
    for copy in copies:
        copy.wait()


def assemble(parts, place):
    length, rank = parts[0].shape
    return pl.pallas_call(
        assemble_kernel,
        out_shape=jax.ShapeDtypeStruct((len(parts) * length, rank), parts[0].dtype),
        in_specs=[pl.BlockSpec(memory_space=pltpu.SMEM)]
        + [pl.BlockSpec(memory_space=pl.ANY)] * len(parts),
        out_specs=pl.BlockSpec(memory_space=pltpu.VMEM),
        scratch_shapes=[pltpu.SemaphoreType.DMA((len(parts),))],
        compiler_params=pltpu.CompilerParams(vmem_limit_bytes=SMALL_KERNEL_BYTES),
        name="assemble",
    )(place[None], *parts)


def forward(delta, right):
    return jnp.dot(delta, right, preferred_element_type=jnp.float32)


def backward(delta, basis):
    total = lax.dot_general(delta, basis, (((0,), (0,)), ((), ())), preferred_element_type=jnp.float32)
    return total.astype(jnp.bfloat16)


def near_parts(share):
    return [share] + [swap(share, "col", mask) for mask in range(2, lax.axis_size("col"), 2)]


def with_other_core(near):
    parts = []
    for part in near:
        parts += [part, swap(part, "col", 1)]
    return parts


def reduce_chips(shares_of, leading):
    bits = chip_bits()

    def step(share, order, turn):
        if not leading:
            return reduce_half(share, "col", order[turn], 0)
        left = sorted(order[turn:], reverse=True)
        dim = left.index(order[turn])
        return lax.squeeze(reduce_half(share, "col", order[turn], dim), (dim,))

    orders = (bits, bits[::-1])
    for m, shares in enumerate(shares_of):
        for turn in range(len(bits)):
            fresh = []
            for share, order in zip(shares, orders):
                fresh.append(step(share, order, turn))
            shares = fresh
        shares_of[m] = shares
    return shares_of


def core_sum(delta, basis):
    bits = chip_bits()
    total = lax.optimization_barrier(backward(delta, basis))
    width = total.shape[0] // lax.axis_size("col")
    total = total.reshape((2,) * len(bits) + (2, width, total.shape[1]))
    return lax.squeeze(reduce_half(total, "col", 1, len(bits)), (len(bits),))


def two_shares(total, dim):
    half = total.shape[dim] // 2
    return [lax.slice_in_dim(total, start, start + half, axis=dim) for start in (0, half)]


def all_columns(deltas, bases):
    bits = chip_bits()
    totals = [reduce_half(backward(delta, basis), "col", 1, 0) for delta, basis in zip(deltas, bases)]
    columns = []
    for shares in reduce_chips([two_shares(total, 0) for total in totals], False):
        value = gather_rows(reduce_rows(jnp.stack(shares), 1).astype(jnp.bfloat16), 1)
        shares = []
        for index, order in ((0, bits[::-1]), (1, bits)):
            share = value[index]
            for bit in order:
                share = gather_half(share, "col", bit, 0)
            shares.append(share)
        columns.append(gather_half(jnp.concatenate(shares, axis=0), "col", 1, 0))
    return columns


def transposed_kernel(*refs):
    out_ref, start = refs[-1], 0
    for ref in refs[:-1]:
        out_ref[:, start : start + ref.shape[0]] = ref[...].T
        start += ref.shape[0]


def transposed(pieces):
    length = sum(piece.shape[0] for piece in pieces)
    return pl.pallas_call(
        transposed_kernel,
        out_shape=jax.ShapeDtypeStruct((pieces[0].shape[1], length), jnp.float32),
        compiler_params=pltpu.CompilerParams(vmem_limit_bytes=SMALL_KERNEL_BYTES),
        name="transposed",
    )(*pieces)


def own_downs(deltas, bases):
    totals = [core_sum(delta, basis.astype(jnp.bfloat16)) for delta, basis in zip(deltas, bases)]
    bases, totals[-1] = lax.optimization_barrier((bases, totals[-1]))
    shares_of = reduce_chips([two_shares(total, total.ndim - 2) for total in totals], True)
    return [reduce_rows(transposed(shares), 0) for shares in shares_of], bases


def extract(base_flat, adjusted_flat, omega):
    matrices, _, _ = omega.shape
    hidden_units = base_flat.shape[1] * lax.axis_size("row") * lax.axis_size("col")
    every = range(matrices)
    near = [near_parts(omega[m]) for m in every]
    deltas = differences(adjusted_flat, base_flat)
    deltas, near = lax.optimization_barrier((deltas, near))
    place = lax.axis_index("col")
    panels = [forward(deltas[m], assemble(with_other_core(near[m]), place)) for m in every]
    inverses = factors(panels)
    first = [product(panels[m], inverses[m], (1, 1)).astype(jnp.bfloat16) for m in every]
    columns = all_columns(deltas, first)
    panels = [forward(deltas[m], columns[m]) for m in every]
    inverses = factors(panels)
    last = [product(panels[m], inverses[m], (1, 1)) for m in every]
    downs, last = own_downs(deltas, last)
    down = jnp.stack(downs).transpose(0, 2, 1)
    up = jnp.stack([math.sqrt(hidden_units) * last[m] for m in every])
    return (up, down)


def solution(mesh):
    in_specs = (P(None, ("row", "col"), None), P(None, ("row", "col"), None), P(None, "col", None))
    out_specs = (P(None, ("row", "col"), None), P(None, "col", "row"))
    return jax.shard_map(extract, mesh=mesh, in_specs=in_specs, out_specs=out_specs, check_vma=False)
```

```python
import math

import jax
import jax.numpy as jnp
from jax import lax
from jax.experimental import pallas as pl
from jax.experimental.pallas import tpu as pltpu
from jax.sharding import PartitionSpec as P


HIGHEST = lax.Precision.HIGHEST
STEP = 64
SMALL_KERNEL_BYTES = 12 << 20
PIVOTS = 4
ROW_TILE = 104


def place_on(axis):
    return lax.axis_index(axis).astype(jnp.uint32)


def bit_of(axis, bit):
    return (place_on(axis) >> jnp.uint32(bit.bit_length() - 1)) & jnp.uint32(1)


def swap(value, axis, mask):
    pairs = [(index, index ^ mask) for index in range(lax.axis_size(axis))]
    return lax.ppermute(value, axis, pairs)


def bits_below(size):
    return [1 << place for place in range(size.bit_length() - 1)]


def half_of(value, which, dim):
    half = value.shape[dim] // 2
    return lax.dynamic_slice_in_dim(value, which * jnp.uint32(half), half, dim)


def reduce_half(value, axis, bit, dim):
    mine = bit_of(axis, bit)
    received = swap(half_of(value, mine ^ jnp.uint32(1), dim).astype(jnp.bfloat16), axis, bit)
    return half_of(value, mine, dim).astype(jnp.float32) + received.astype(jnp.float32)


def gather_half(value, axis, bit, dim):
    mine = bit_of(axis, bit)
    received = swap(value, axis, bit)
    low = jnp.where(mine == 0, value, received)
    high = jnp.where(mine == 0, received, value)
    return jnp.concatenate([low, high], axis=dim)


def arrange(parts, place):
    for bit in bits_below(len(parts)):
        odd = (place & jnp.uint32(bit)) != 0
        fresh = list(parts)
        for i in range(len(parts)):
            if not i & bit:
                fresh[i] = jnp.where(odd, parts[i | bit], parts[i])
                fresh[i | bit] = jnp.where(odd, parts[i], parts[i | bit])
        parts = fresh
    return parts


def chip_bits():
    return bits_below(lax.axis_size("col"))[1:]


def reduce_rows(value, dim):
    rows = lax.axis_size("row")
    place = place_on("row")
    size = value.shape[dim] // rows

    def part(owner):
        return lax.dynamic_slice_in_dim(value, owner * jnp.uint32(size), size, dim)

    total = [part(place)]
    for mask in range(1, rows):
        sent = part(place ^ jnp.uint32(mask)).astype(jnp.bfloat16)
        total.append(swap(sent, "row", mask).astype(jnp.float32))
    return tree_sum(total)


def gather_rows(value, dim):
    rows = lax.axis_size("row")
    parts = [value] + [swap(value, "row", mask) for mask in range(1, rows)]
    return jnp.concatenate(arrange(parts, place_on("row")), axis=dim)


def tree_sum(parts):
    while len(parts) > 1:
        parts = [parts[i] + parts[i + 1] for i in range(0, len(parts), 2)]
    return parts[0]


def eliminate(block, row, j):
    columns = [jnp.broadcast_to(block[:, j + i : j + i + 1], block.shape) for i in range(PIVOTS)]
    rows = [block[j + i : j + i + 1, :] for i in range(PIVOTS)]
    corner = [[columns[k][j + i : j + i + 1, :] for k in range(PIVOTS)] for i in range(PIVOTS)]
    for i in range(PIVOTS):
        scale = 1.0 / corner[i][i]
        block = block - jnp.where(row > j + i, columns[i], 0.0) * (rows[i] * scale)
        for k in range(i + 1, PIVOTS):
            ratio = corner[k][i] * scale
            rows[k] = rows[k] - ratio * rows[i]
            columns[k] = columns[k] - columns[i] * ratio
            for l in range(k, PIVOTS):
                corner[l][k] = corner[l][k] - corner[l][i] * ratio
    return block


def inverse_factor_kernel(gram_ref, inverse_ref, work_ref):
    count, rank, _ = gram_ref.shape
    step = min(STEP, rank)
    row = lax.broadcasted_iota(jnp.int32, (step, 2 * step), 0)
    lane = lax.broadcasted_iota(jnp.int32, (step, 2 * step), 1)
    eye = jnp.where(lane == row + step, 1.0, 0.0)[:, step:]
    full = lax.broadcasted_iota(jnp.int32, (step, rank), 1)
    for m in range(count):
        work_ref[m] = gram_ref[m]
    for start in range(0, rank, step):
        stop = start + step
        blocks = [
            jnp.concatenate([work_ref[m, start:stop, start:stop], eye], axis=1)
            for m in range(count)
        ]
        for j in range(0, step, PIVOTS):
            for m in range(count):
                blocks[m] = eliminate(blocks[m], row, j)
        for m in range(count):
            block = blocks[m]
            diagonal = jnp.sum(jnp.where(lane == row, block, 0.0), axis=1, keepdims=True)
            inverse = block[:, step:] * lax.rsqrt(diagonal)
            unit = [jnp.zeros((step, start), jnp.float32)] if start else []
            unit += [eye]
            unit += [jnp.zeros((step, rank - stop), jnp.float32)] if stop < rank else []
            unit = jnp.concatenate(unit, axis=1) if len(unit) > 1 else unit[0]
            panel = jnp.where((full >= start) & (full < stop), unit, work_ref[m, start:stop, :])
            solved = jnp.dot(inverse, panel, precision=HIGHEST, preferred_element_type=jnp.float32)
            inverse_ref[m, start:stop, :] = jnp.where(full < stop, solved, 0.0)
            if stop < rank:
                rest = work_ref[m, stop:, :]
                wide = lax.broadcasted_iota(jnp.int32, rest.shape, 1)
                rest = jnp.where((wide >= start) & (wide < stop), 0.0, rest)
                work_ref[m, stop:, :] = rest - lax.dot_general(
                    solved[:, stop:],
                    solved,
                    (((0,), (0,)), ((), ())),
                    precision=HIGHEST,
                    preferred_element_type=jnp.float32,
                )


def inverse_factor(gram):
    return pl.pallas_call(
        inverse_factor_kernel,
        out_shape=jax.ShapeDtypeStruct(gram.shape, jnp.float32),
        scratch_shapes=[pltpu.VMEM(gram.shape, jnp.float32)],
        compiler_params=pltpu.CompilerParams(vmem_limit_bytes=SMALL_KERNEL_BYTES),
        name="inverse_factor",
    )(gram)


def sum_everywhere(gram):
    columns = lax.axis_size("col")
    rows = lax.axis_size("row")
    chips = columns // 2
    mine = bit_of("col", 1)
    chip = place_on("col") >> jnp.uint32(1)
    value = half_of(gram, mine, 1) + swap(half_of(gram, mine ^ jnp.uint32(1), 1), "col", 1)
    chunk = value.shape[1] // chips

    def part(owner):
        return lax.dynamic_slice_in_dim(value, owner * jnp.uint32(chunk), chunk, 1)

    parts = [part(chip)]
    for mask in range(1, chips):
        parts.append(swap(part(chip ^ jnp.uint32(mask)), "col", 2 * mask))
    value = tree_sum(parts)
    value = tree_sum([value] + [swap(value, "row", mask) for mask in range(1, rows)])
    parts = [value] + [swap(value, "col", 2 * mask) for mask in range(1, chips)]
    whole = jnp.concatenate(arrange(parts, chip), axis=1)
    return gather_half(whole, "col", 1, 1)


def product(left, right, dims):
    dims = ((dims[:1], dims[1:]), ((), ()))
    return lax.dot_general(left, right, dims, precision=HIGHEST, preferred_element_type=jnp.float32)


def factors(panels):
    grams = jnp.stack([product(panel, panel, (0, 0)) for panel in panels])
    return inverse_factor(sum_everywhere(grams))


def difference_kernel(adjusted_ref, base_ref, *delta_refs):
    wide = adjusted_ref[...].astype(jnp.float32) - base_ref[...].astype(jnp.float32)
    wide = jnp.swapaxes(wide, 0, 1)
    for m, delta_ref in enumerate(delta_refs):
        delta_ref[...] = wide[m].astype(jnp.bfloat16)


def differences(adjusted, base):
    matrices, rows, width = base.shape
    tall = min(ROW_TILE, rows)
    stacked = pl.BlockSpec((tall, matrices, width), lambda i: (i, 0, 0))
    return pl.pallas_call(
        difference_kernel,
        out_shape=(jax.ShapeDtypeStruct((rows, width), jnp.bfloat16),) * matrices,
        grid=(pl.cdiv(rows, tall),),
        in_specs=[stacked, stacked],
        out_specs=(pl.BlockSpec((tall, width), lambda i: (i, 0)),) * matrices,
        name="difference",
    )(adjusted.transpose(1, 0, 2), base.transpose(1, 0, 2))


def assemble_kernel(place_ref, *refs):
    *part_refs, out_ref, sems = refs
    length = part_refs[0].shape[0]
    copies = []
    for index, part_ref in enumerate(part_refs):
        start = pl.multiple_of((place_ref[0] ^ index) * length, length)
        copies.append(pltpu.make_async_copy(part_ref, out_ref.at[pl.ds(start, length), :], sems.at[index]))
    for copy in copies:
        copy.start()
    for copy in copies:
        copy.wait()


def assemble(parts, place):
    length, rank = parts[0].shape
    return pl.pallas_call(
        assemble_kernel,
        out_shape=jax.ShapeDtypeStruct((len(parts) * length, rank), parts[0].dtype),
        in_specs=[pl.BlockSpec(memory_space=pltpu.SMEM)]
        + [pl.BlockSpec(memory_space=pl.ANY)] * len(parts),
        out_specs=pl.BlockSpec(memory_space=pltpu.VMEM),
        scratch_shapes=[pltpu.SemaphoreType.DMA((len(parts),))],
        compiler_params=pltpu.CompilerParams(vmem_limit_bytes=SMALL_KERNEL_BYTES),
        name="assemble",
    )(place[None], *parts)


def forward(delta, right):
    return jnp.dot(delta, right, preferred_element_type=jnp.float32)


def backward(delta, basis):
    total = lax.dot_general(delta, basis, (((0,), (0,)), ((), ())), preferred_element_type=jnp.float32)
    return total.astype(jnp.bfloat16)


def near_parts(share):
    return [share] + [swap(share, "col", mask) for mask in range(2, lax.axis_size("col"), 2)]


def with_other_core(near):
    parts = []
    for part in near:
        parts += [part, swap(part, "col", 1)]
    return parts


def reduce_chips(shares_of, leading):
    bits = chip_bits()

    def step(share, order, turn):
        if not leading:
            return reduce_half(share, "col", order[turn], 0)
        left = sorted(order[turn:], reverse=True)
        dim = left.index(order[turn])
        return lax.squeeze(reduce_half(share, "col", order[turn], dim), (dim,))

    orders = (bits, bits[::-1])
    for m, shares in enumerate(shares_of):
        for turn in range(len(bits)):
            fresh = []
            for share, order in zip(shares, orders):
                fresh.append(step(share, order, turn))
            shares = fresh
        shares_of[m] = shares
    return shares_of


def core_sum(delta, basis):
    bits = chip_bits()
    total = lax.optimization_barrier(backward(delta, basis))
    width = total.shape[0] // lax.axis_size("col")
    total = total.reshape((2,) * len(bits) + (2, width, total.shape[1]))
    return lax.squeeze(reduce_half(total, "col", 1, len(bits)), (len(bits),))


def two_shares(total, dim):
    half = total.shape[dim] // 2
    return [lax.slice_in_dim(total, start, start + half, axis=dim) for start in (0, half)]


def all_columns(deltas, bases):
    bits = chip_bits()
    totals = [reduce_half(backward(delta, basis), "col", 1, 0) for delta, basis in zip(deltas, bases)]
    columns = []
    shares_of = reduce_chips([two_shares(total, 0) for total in totals], False)
    for shares in shares_of:
        value = reduce_rows(jnp.stack(shares), 1)
        value = gather_rows(value.astype(jnp.bfloat16), 1)
        shares = []
        for index, order in ((0, bits[::-1]), (1, bits)):
            share = value[index]
            for bit in order:
                share = gather_half(share, "col", bit, 0)
            shares.append(share)
        columns.append(gather_half(jnp.concatenate(shares, axis=0), "col", 1, 0))
    return columns


def transposed_kernel(*refs):
    out_ref, start = refs[-1], 0
    for ref in refs[:-1]:
        out_ref[:, start : start + ref.shape[0]] = ref[...].T
        start += ref.shape[0]


def transposed(pieces):
    length = sum(piece.shape[0] for piece in pieces)
    return pl.pallas_call(
        transposed_kernel,
        out_shape=jax.ShapeDtypeStruct((pieces[0].shape[1], length), jnp.float32),
        compiler_params=pltpu.CompilerParams(vmem_limit_bytes=SMALL_KERNEL_BYTES),
        name="transposed",
    )(*pieces)


def own_downs(deltas, bases):
    totals = [core_sum(delta, basis.astype(jnp.bfloat16)) for delta, basis in zip(deltas, bases)]
    bases, totals[-1] = lax.optimization_barrier((bases, totals[-1]))
    shares_of = reduce_chips([two_shares(total, total.ndim - 2) for total in totals], True)
    downs = []
    for shares in shares_of:
        downs.append(reduce_rows(transposed(shares), 0))
    return downs, bases


def extract(base_flat, adjusted_flat, omega):
    matrices, _, _ = omega.shape
    hidden_units = base_flat.shape[1] * lax.axis_size("row") * lax.axis_size("col")
    every = range(matrices)
    near = []
    for m in every:
        near.append(near_parts(omega[m]))
    deltas = differences(adjusted_flat, base_flat)
    deltas, near[0] = lax.optimization_barrier((deltas, near[0]))
    place = lax.axis_index("col")
    panels = []
    for m in every:
        parts = with_other_core(near[m])
        right = assemble(parts, place)
        panels.append(forward(deltas[m], right))
    inverses = factors(panels)
    first = [product(panels[m], inverses[m], (1, 1)).astype(jnp.bfloat16) for m in every]
    columns = all_columns(deltas, first)
    panels = [forward(deltas[m], columns[m]) for m in every]
    inverses = factors(panels)
    last = [product(panels[m], inverses[m], (1, 1)) for m in every]
    downs, last = own_downs(deltas, last)
    down = jnp.stack(downs).transpose(0, 2, 1)
    up = jnp.stack([math.sqrt(hidden_units) * last[m] for m in every])
    return (up, down)


def solution(mesh):
    in_specs = (P(None, ("row", "col"), None), P(None, ("row", "col"), None), P(None, "col", None))
    out_specs = (P(None, ("row", "col"), None), P(None, "col", "row"))
    return jax.shard_map(extract, mesh=mesh, in_specs=in_specs, out_specs=out_specs, check_vma=False)
```
